512 devices in a mesh: gx: 8 (over y, z_hi), gy: 8 (over z_lo), gz: 8 (over x, core).
Axes of the slice: x: 4, y: 4, z: 16 (z_hi: 2, z_lo: 8; z = z_hi * 8 + z_lo), core: 2. Of those that a mesh axis runs over, the one named last changes fastest.
Arguments:
- tokens: bfloat16 [1024, 8192], P('gx', 'gz'), may hold values from -6 to 6
- gate_weight: bfloat16 [8192, 14336], P('gz', ('gx', 'gy')), may hold values from -0.0625 to 0.0625
- up_weight: bfloat16 [8192, 14336], P('gz', ('gx', 'gy')), may hold values from -0.0625 to 0.0625
- down_weight: bfloat16 [14336, 8192], P(('gx', 'gy'), 'gz'), may hold values from -0.046875 to 0.046875
- out_grad: bfloat16 [1024, 8192], P('gx', 'gz'), may hold values from -6 to 6
Outputs:
- output: bfloat16 [1024, 8192], P('gx', 'gz')
- input_grad: bfloat16 [1024, 8192], P('gx', 'gz')
- gate_grad: bfloat16 [8192, 14336], P('gz', ('gx', 'gy'))
- up_grad: bfloat16 [8192, 14336], P('gz', ('gx', 'gy'))
- down_grad: bfloat16 [14336, 8192], P(('gx', 'gy'), 'gz')
The draws below stay inside these ranges and needn't reach their ends.
All inputs are finite; a program needn't handle non-finite values.
Results may differ from the reference program's by a relative error of at most 0.025.
Values may be sent and summed in bfloat16 or wider, within the bound.
No kernel may reach another device: no remote copies, remote signals or barrier semaphores. Data moves between devices by JAX's collectives and lax.ppermute only.
A program may use at most 64 MiB of HBM per device.

```python
import jax
import jax.numpy as jnp
from jax import lax

D = 8192
FF = 14336
TOKENS = 1024
N_GX = 8
N_GY = 8
N_GZ = 8


def block_scale(rng, extent, pieces, least, largest):
    factor_of = 1.0
    for axis_at, parts in pieces:
        steps = jax.random.uniform(jax.random.fold_in(jax.random.fold_in(rng, 6), axis_at), (parts,), jnp.float32, least / len(pieces), largest / len(pieces))
        factor_of = factor_of * jnp.repeat(jnp.exp(steps), extent[axis_at] // parts).reshape((-1,) + (1,) * (len(extent) - 1 - axis_at))
    return factor_of


def scatter_about(key, shape, scale, bound, pieces=(), kind=jnp.bfloat16):
    drawn = jax.random.normal(key, shape, jnp.float32) * scale
    if len(pieces) > 0:
        drawn = block_scale(key, shape, pieces, -0.22, 0.18) * drawn
    return jnp.clip(drawn, min=-bound, max=bound).astype(kind)


def setup_inputs(seed: int = 0) -> dict:
    key_of = jax.random.split(jax.random.key(seed), 6)
    return {
        "tokens": scatter_about(key_of[0], (TOKENS, D), 1.0, 6.0, ((0, 8), (1, 8))),
        "gate_weight": scatter_about(key_of[1], (D, FF), D ** -0.5, 0.0625, ((0, 8), (1, 64))),
        "up_weight": scatter_about(key_of[2], (D, FF), D ** -0.5, 0.0625, ((0, 8), (1, 64))),
        "down_weight": scatter_about(key_of[3], (FF, D), FF ** -0.5, 0.046875, ((0, 64), (1, 8))),
        "out_grad": scatter_about(key_of[4], (TOKENS, D), 1.0, 6.0, ((0, 8), (1, 8))),
    }


def contract_rows(left, right):
    return lax.dot_general(left, right, (((0,), (0,)), ((), ())), preferred_element_type=jnp.float32)


def contract_cols(left, right):
    return lax.dot_general(left, right, (((1,), (1,)), ((), ())), preferred_element_type=jnp.float32)


def reference(tokens, gate_weight, up_weight, down_weight, out_grad):
    feature_width = D // N_GZ

    def gate_block(carry, block_index):
        offset = (block_index * feature_width).astype(jnp.int32)
        rows = lax.dynamic_slice_in_dim(tokens, offset, feature_width, 1)
        gate_rows = lax.dynamic_slice_in_dim(gate_weight, offset, feature_width, 0)
        up_rows = lax.dynamic_slice_in_dim(up_weight, offset, feature_width, 0)
        gate_term = jnp.dot(rows, gate_rows, preferred_element_type=jnp.float32)
        up_term = jnp.dot(rows, up_rows, preferred_element_type=jnp.float32)
        gate_term = lax.optimization_barrier(gate_term.astype(jnp.bfloat16)).astype(jnp.float32)
        up_term = lax.optimization_barrier(up_term.astype(jnp.bfloat16)).astype(jnp.float32)
        return (carry[0] + gate_term, carry[1] + up_term), None

    empty = jnp.zeros((tokens.shape[0], FF), jnp.float32)
    (gate, upward), _ = lax.scan(gate_block, (empty, empty), jnp.arange(N_GZ, dtype=jnp.int32))
    sigmoid = jax.nn.sigmoid(gate)
    hidden = (gate * sigmoid * upward).astype(jnp.bfloat16)
    output = jnp.dot(hidden, down_weight, preferred_element_type=jnp.float32).astype(jnp.bfloat16)
    dhidden = contract_cols(out_grad, down_weight)
    dgate = (dhidden * upward * sigmoid * (1.0 + gate * (1.0 - sigmoid))).astype(jnp.bfloat16)
    dupward = (dhidden * gate * sigmoid).astype(jnp.bfloat16)
    hidden_width = FF // (N_GX * N_GY)

    def input_block(carry, block_index):
        offset = (block_index * hidden_width).astype(jnp.int32)
        grad_gate = lax.dynamic_slice_in_dim(dgate, offset, hidden_width, 1)
        grad_up = lax.dynamic_slice_in_dim(dupward, offset, hidden_width, 1)
        gate_cols = lax.dynamic_slice_in_dim(gate_weight, offset, hidden_width, 1)
        up_cols = lax.dynamic_slice_in_dim(up_weight, offset, hidden_width, 1)
        term = contract_cols(grad_gate, gate_cols) + contract_cols(grad_up, up_cols)
        term = lax.optimization_barrier(term.astype(jnp.bfloat16)).astype(jnp.float32)
        return carry + term, None

    zeros_in = jnp.zeros((tokens.shape[0], D), jnp.float32)
    input_sum, _ = lax.scan(input_block, zeros_in, jnp.arange(N_GX * N_GY, dtype=jnp.int32))
    input_grad = input_sum.astype(jnp.bfloat16)
    gate_grad = contract_rows(tokens, dgate).astype(jnp.bfloat16)
    up_grad = contract_rows(tokens, dupward).astype(jnp.bfloat16)
    down_grad = contract_rows(hidden, out_grad).astype(jnp.bfloat16)
    return (output, input_grad, gate_grad, up_grad, down_grad)
```

```python
import jax
import jax.numpy as jnp
from jax import lax
from jax.sharding import Mesh
from jax.sharding import PartitionSpec as P

GZ = ("x", "c")
Z = ("zh", "zl")


def give_all(shard, axis):
    devices = lax.axis_size(axis)
    return lax.all_to_all(
        jnp.broadcast_to(shard[None], (devices, *shard.shape)), axis, 0, 0, tiled=True
    )


def exchange(tiles, axis):
    return lax.all_to_all(tiles, axis, 0, 0, tiled=True)


def total(tiles):
    return jnp.sum(tiles.astype(jnp.float32), axis=0)


def contract_rows(left, right):
    return lax.dot_general(
        left, right, (((0,), (0,)), ((), ())), preferred_element_type=jnp.float32
    )


def contract_cols(left, right):
    return lax.dot_general(
        left, right, (((1,), (1,)), ((), ())), preferred_element_type=jnp.float32
    )


def matmul(left, right):
    return jnp.dot(left, right, preferred_element_type=jnp.float32)


def finish(part):
    halves, ys, rows, width = part.shape
    by_y = exchange(jnp.swapaxes(part, 0, 1), "y")
    mine = total(by_y).astype(jnp.bfloat16)
    mine = jnp.where(lax.axis_index("zh") == 0, mine, mine[::-1])
    zl = lax.axis_size("zl")
    pieces = exchange(mine.reshape(halves * zl, rows // zl, width), Z)
    return give_all(total(pieces).astype(jnp.bfloat16), "zl").reshape(rows, width)


def body(tokens, gate_weight, up_weight, down_weight, out_grad):
    rows, width = tokens.shape
    hid = down_weight.shape[0]
    zl = lax.axis_size("zl")
    nz = 2 * zl
    cut = rows // zl
    at = lax.axis_index("zl") * cut
    own_tokens = give_all(tokens, "y").reshape(-1, width)
    thin = jnp.concatenate(
        [lax.dynamic_slice_in_dim(a, at, cut, 0) for a in (tokens, out_grad)], axis=0
    )
    far = lax.ppermute(thin, Z, [(i, (i + zl) % nz) for i in range(nz)])
    far_tokens = give_all(far[:cut], "zl").reshape(rows, width)
    far_tokens = give_all(far_tokens, "y").reshape(-1, width)
    own_grad = give_all(out_grad, "y").reshape(-1, width)
    far_grad = give_all(far[cut:], "zl").reshape(rows, width)
    far_grad = give_all(far_grad, "y").reshape(-1, width)

    def up_terms(some):
        return jnp.concatenate(
            [matmul(some, w).astype(jnp.bfloat16) for w in (gate_weight, up_weight)], axis=1
        )

    def spread(own, other):
        both = jnp.concatenate([own, other], axis=0)
        return both.reshape(8, -1, both.shape[1])

    pre = total(exchange(spread(up_terms(own_tokens), up_terms(far_tokens)), GZ))
    gate, upward = pre[:, :hid], pre[:, hid:]
    sigmoid = jax.nn.sigmoid(gate)
    hidden = (gate * sigmoid * upward).astype(jnp.bfloat16)
    hidden_all = give_all(hidden, GZ).reshape(-1, hid)
    output = finish(
        matmul(hidden_all, down_weight).astype(jnp.bfloat16).reshape(2, -1, rows, width)
    )
    dhidden = total(
        exchange(
            spread(
                contract_cols(own_grad, down_weight).astype(jnp.bfloat16),
                contract_cols(far_grad, down_weight).astype(jnp.bfloat16),
            ),
            GZ,
        )
    )
    dgate = (dhidden * upward * sigmoid * (1.0 + gate * (1.0 - sigmoid))).astype(jnp.bfloat16)
    dup = (dhidden * gate * sigmoid).astype(jnp.bfloat16)
    both = give_all(jnp.concatenate([dgate, dup], axis=1), GZ).reshape(-1, 2 * hid)
    dgate_all, dup_all = both[:, :hid], both[:, hid:]
    input_part = contract_cols(dgate_all, gate_weight) + contract_cols(dup_all, up_weight)
    input_grad = finish(input_part.astype(jnp.bfloat16).reshape(2, -1, rows, width))
    all_tokens = jnp.concatenate([own_tokens, far_tokens], axis=0)
    all_grad = jnp.concatenate([own_grad, far_grad], axis=0)
    gate_grad = contract_rows(all_tokens, dgate_all).astype(jnp.bfloat16)
    up_grad = contract_rows(all_tokens, dup_all).astype(jnp.bfloat16)
    down_grad = contract_rows(hidden_all, all_grad).astype(jnp.bfloat16)
    return (output, input_grad, gate_grad, up_grad, down_grad)


def solution(mesh):
    finer = Mesh(
        mesh.devices.reshape(4, 2, mesh.shape["gy"], 4, 2), ("y", "zh", "zl", "x", "c")
    )
    gx, ff = ("y", "zh"), ("y", "zh", "zl")
    in_specs = (P(gx, GZ), P(GZ, ff), P(GZ, ff), P(ff, GZ), P(gx, GZ))
    out_specs = (P(gx, GZ), P(gx, GZ), P(GZ, ff), P(GZ, ff), P(ff, GZ))
    return jax.shard_map(body, mesh=finer, in_specs=in_specs, out_specs=out_specs, check_vma=False)
```

```python
import jax
import jax.numpy as jnp
from jax import lax
from jax.experimental import pallas as pl
from jax.experimental.pallas import tpu as pltpu
from jax.sharding import Mesh
from jax.sharding import PartitionSpec as P

GZ = ("x", "c")
Z = ("zh", "zl")
HALVING = (0, 1, 2)
LANES = 256


def give_all(shard, axis):
    devices = lax.axis_size(axis)
    return lax.all_to_all(
        jnp.broadcast_to(shard[None], (devices, *shard.shape)), axis, 0, 0, tiled=True
    )


def exchange(tiles, axis):
    return lax.all_to_all(tiles, axis, 0, 0, tiled=True)


def total(tiles):
    return jnp.sum(tiles.astype(jnp.float32), axis=0)


def to_y(block, d):
    n = lax.axis_size("y")
    return lax.ppermute(block, "y", [(i, (i + d) % n) for i in range(n)])


def of_ys(shard):
    blocks = [shard]
    for d in (1, 2, 3):
        blocks.append(to_y(shard, -d))
    return blocks


def across(shard):
    zl = lax.axis_size("zl")
    nz, step = 2 * zl, zl // 2
    return lax.ppermute(
        shard, Z, [(i, (i - step if i % zl < step else i + step) % nz) for i in range(nz)]
    )


def to_bit(block, bit):
    return lax.ppermute(block, "zl", [(i, i ^ (1 << bit)) for i in range(lax.axis_size("zl"))])


def halved(tiles, bit):
    pairs = tiles.reshape(-1, 2, *tiles.shape[1:])
    got = to_bit(pairs[:, 1], bit)
    return pairs[:, 0].astype(jnp.float32) + got.astype(jnp.float32)


def contract_rows(left, right):
    return lax.dot_general(
        left, right, (((0,), (0,)), ((), ())), preferred_element_type=jnp.float32
    )


def contract_cols(left, right):
    return lax.dot_general(
        left, right, (((1,), (1,)), ((), ())), preferred_element_type=jnp.float32
    )


def matmul(left, right):
    return jnp.dot(left, right, preferred_element_type=jnp.float32)


def own_kernel(zl, tokens, grad, out):
    for r in range(out.shape[0]):
        s = jnp.bitwise_xor(zl[0], r)
        out[r, 0] = tokens[s]
        out[r, 1] = grad[s]


def terms_kernel(b0, b1, b2, b3, wide, down, out):
    n, _, cut, width = b0.shape
    rows = n * cut
    for k, b in enumerate((b0, b1, b2, b3)):
        t = b[:, 0].reshape(rows, width)
        g = b[:, 1].reshape(rows, width)
        at = pl.ds(k * rows, rows)
        out[at, : 2 * LANES] = matmul(t, wide[...]).astype(jnp.bfloat16)
        out[at, 2 * LANES :] = contract_cols(g, down[...]).astype(jnp.bfloat16)


def leave_kernel(acts, wide, down, *outs):
    rows = acts.shape[0] // 4
    n, _, cut, width = outs[0].shape
    for d, out in enumerate(outs):
        at = pl.ds(d * rows, rows)
        o = matmul(acts[at, :LANES], down[...]).astype(jnp.bfloat16)
        out[:, 0] = o.reshape(n, cut, width)
        i = contract_cols(acts[at, LANES:], wide[...]).astype(jnp.bfloat16)
        out[:, 1] = i.reshape(n, cut, width)


def sum_kernel(a, b, c, d, out):
    f32 = jnp.float32
    out[...] = (
        a[...].astype(f32) + b[...].astype(f32) + c[...].astype(f32) + d[...].astype(f32)
    ).astype(jnp.bfloat16)


def work(tokens, gate_weight, up_weight, down_weight, out_grad):
    rows, width = tokens.shape
    hid = down_weight.shape[0]
    zl = lax.axis_size("zl")
    cut = rows // zl
    block = jax.ShapeDtypeStruct((zl, 2, cut, width), jnp.bfloat16)
    more = LANES - hid
    vmem = pl.BlockSpec(memory_space=pltpu.VMEM)
    own = pl.pallas_call(
        own_kernel,
        out_shape=block,
        in_specs=[pl.BlockSpec(memory_space=pltpu.SMEM), vmem, vmem],
        name="own",
    )(
        lax.axis_index("zl").astype(jnp.int32).reshape(1),
        *(a.reshape(zl, cut, width) for a in (tokens, out_grad)),
    )
    wide = jnp.concatenate(
        [jnp.pad(w, ((0, 0), (0, more))) for w in (gate_weight, up_weight)], axis=1
    )
    down = jnp.pad(down_weight, ((0, more), (0, 0)))
    far = across(own[:1])
    own = of_ys(own)
    for bit in HALVING[::-1]:
        got = to_bit(far, bit)
        far = jnp.stack([far, got], axis=1).reshape(-1, *far.shape[1:])
    far = of_ys(far)

    def terms(blocks):
        made = pl.pallas_call(
            terms_kernel,
            out_shape=jax.ShapeDtypeStruct((4 * rows, 3 * LANES), jnp.bfloat16),
            name="terms",
        )(*blocks, wide, down)
        made = exchange(made.reshape(8, rows // 2, -1), GZ)
        return total(made)

    def gates(pre):
        gate, upward, dhidden = (pre[:, k * LANES : (k + 1) * LANES] for k in range(3))
        sigmoid = jax.nn.sigmoid(gate)
        hidden = (gate * sigmoid * upward).astype(jnp.bfloat16)
        dgate = (dhidden * upward * sigmoid * (1.0 + gate * (1.0 - sigmoid))).astype(jnp.bfloat16)
        dup = (dhidden * gate * sigmoid).astype(jnp.bfloat16)
        acts = jnp.concatenate([hidden, dgate, dup], axis=1)
        acts = give_all(acts, GZ)
        return acts.reshape(4 * rows, -1)

    def leave(acts):
        parts = pl.pallas_call(leave_kernel, out_shape=[block] * 4, name="leave")(acts, wide, down)
        back = [to_y(parts[d], d) for d in (1, 2, 3)]
        mine = pl.pallas_call(sum_kernel, out_shape=block, name="add")(parts[0], *back)
        return mine

    own_acts = gates(terms(own))
    far_acts = gates(terms(far))
    own_sum = leave(own_acts)
    far_sum = leave(far_acts)
    for bit in HALVING:
        own_sum = halved(own_sum.astype(jnp.bfloat16), bit)
        far_sum = halved(far_sum.astype(jnp.bfloat16), bit)
    own_sum, far_sum = own_sum[0], far_sum[0].astype(jnp.bfloat16)
    far_sum = across(far_sum)
    ends = (own_sum + far_sum.astype(jnp.float32)).astype(jnp.bfloat16)
    ends = give_all(ends, "zl")
    output, input_grad = (ends[:, k].reshape(rows, width) for k in range(2))

    all_tokens, all_grad = (
        jnp.concatenate([b[:, k].reshape(rows, width) for b in own + far], axis=0)
        for k in range(2)
    )
    acts = jnp.concatenate([own_acts, far_acts], axis=0)
    hidden, dgate, dup = (acts[:, k * LANES : k * LANES + hid] for k in range(3))
    gate_grad = contract_rows(all_tokens, dgate).astype(jnp.bfloat16)
    up_grad = contract_rows(all_tokens, dup).astype(jnp.bfloat16)
    down_grad = contract_rows(hidden, all_grad).astype(jnp.bfloat16)
    return (output, input_grad, gate_grad, up_grad, down_grad)


def solution(mesh):
    finer = Mesh(
        mesh.devices.reshape(4, 2, mesh.shape["gy"], 4, 2), ("y", "zh", "zl", "x", "c")
    )
    gx, ff = ("y", "zh"), ("y", "zh", "zl")
    in_specs = (P(gx, GZ), P(GZ, ff), P(GZ, ff), P(ff, GZ), P(gx, GZ))
    out_specs = (P(gx, GZ), P(gx, GZ), P(GZ, ff), P(GZ, ff), P(ff, GZ))
    return jax.shard_map(work, mesh=finer, in_specs=in_specs, out_specs=out_specs, check_vma=False)
```

```python
import jax
import jax.numpy as jnp
from jax import lax
from jax.experimental import pallas as pl
from jax.experimental.pallas import tpu as pltpu
from jax.sharding import Mesh
from jax.sharding import PartitionSpec as P

GZ = ("x", "c")
Z = ("zh", "zl")
HALVING = (0, 1, 2)
LANES = 256


def give_all(shard, axis):
    devices = lax.axis_size(axis)
    return lax.all_to_all(
        jnp.broadcast_to(shard[None], (devices, *shard.shape)), axis, 0, 0, tiled=True
    )


def exchange(tiles, axis):
    return lax.all_to_all(tiles, axis, 0, 0, tiled=True)


def total(tiles):
    return jnp.sum(tiles.astype(jnp.float32), axis=0)


def to_y(block, d):
    n = lax.axis_size("y")
    return lax.ppermute(block, "y", [(i, (i + d) % n) for i in range(n)])


def of_ys(shard):
    blocks = [shard]
    for d in (1, 2, 3):
        blocks.append(to_y(shard, -d))
    return blocks


def across(shard):
    zl = lax.axis_size("zl")
    nz, step = 2 * zl, zl // 2
    return lax.ppermute(
        shard, Z, [(i, (i - step if i % zl < step else i + step) % nz) for i in range(nz)]
    )


def to_bit(block, bit):
    return lax.ppermute(block, "zl", [(i, i ^ (1 << bit)) for i in range(lax.axis_size("zl"))])


def halved(keep, send, bit):
    got = to_bit(send, bit)
    return keep.astype(jnp.float32) + got.astype(jnp.float32)


def contract_rows(left, right):
    return lax.dot_general(
        left, right, (((0,), (0,)), ((), ())), preferred_element_type=jnp.float32
    )


def contract_cols(left, right):
    return lax.dot_general(
        left, right, (((1,), (1,)), ((), ())), preferred_element_type=jnp.float32
    )


def matmul(left, right):
    return jnp.dot(left, right, preferred_element_type=jnp.float32)


def own_kernel(zl, tokens, grad, out, thin):
    for p, r in enumerate((0, 2, 4, 6, 1, 3, 5, 7)):
        s = jnp.bitwise_xor(zl[0], r)
        out[p, 0] = tokens[s]
        out[p, 1] = grad[s]
    thin[0, 0] = tokens[zl[0]]
    thin[0, 1] = grad[zl[0]]


def terms_kernel(*refs):
    *blocks, wide, down, out, t, g = refs
    at = 0
    for b in blocks:
        n, _, cut, width = b.shape
        rows = pl.ds(at, n * cut)
        t[rows] = b[:, 0].reshape(n * cut, width)
        g[rows] = b[:, 1].reshape(n * cut, width)
        at += n * cut
    out[:, : 2 * LANES] = matmul(t[...], wide[...]).astype(jnp.bfloat16)
    out[:, 2 * LANES :] = contract_cols(g[...], down[...]).astype(jnp.bfloat16)


def leave_kernel(acts, wide, down, *outs):
    o = matmul(acts[:, :LANES], down[...]).astype(jnp.bfloat16)
    i = contract_cols(acts[:, LANES:], wide[...]).astype(jnp.bfloat16)
    at = 0
    for out in outs:
        n, _, cut, width = out.shape
        out[:, 0] = o[at : at + n * cut].reshape(n, cut, width)
        out[:, 1] = i[at : at + n * cut].reshape(n, cut, width)
        at += n * cut


def sum_kernel(*refs):
    *terms, even, odd = refs
    half = even.shape[0]
    for out, at in ((even, 0), (odd, half)):
        rows = pl.ds(at, half)
        out[...] = sum(t[rows].astype(jnp.float32) for t in terms).astype(jnp.bfloat16)


def add(*terms):
    n, *rest = terms[0].shape
    shape = jax.ShapeDtypeStruct((n // 2, *rest), jnp.bfloat16)
    return pl.pallas_call(sum_kernel, out_shape=[shape] * 2, name="add")(*terms)


def work(tokens, gate_weight, up_weight, down_weight, out_grad):
    rows, width = tokens.shape
    hid = down_weight.shape[0]
    zl = lax.axis_size("zl")
    cut = rows // zl
    block = jax.ShapeDtypeStruct((zl, 2, cut, width), jnp.bfloat16)
    more = LANES - hid
    vmem = pl.BlockSpec(memory_space=pltpu.VMEM)
    own, thin = pl.pallas_call(
        own_kernel,
        out_shape=[block, jax.ShapeDtypeStruct((1, *block.shape[1:]), jnp.bfloat16)],
        in_specs=[pl.BlockSpec(memory_space=pltpu.SMEM), vmem, vmem],
        name="own",
    )(
        lax.axis_index("zl").astype(jnp.int32).reshape(1),
        *(a.reshape(zl, cut, width) for a in (tokens, out_grad)),
    )
    wide = jnp.concatenate(
        [jnp.pad(w, ((0, 0), (0, more))) for w in (gate_weight, up_weight)], axis=1
    )
    down = jnp.pad(down_weight, ((0, more), (0, 0)))
    far = across(thin)
    own = of_ys(own)
    for bit in HALVING[:0:-1]:
        got = to_bit(far, bit)
        far = jnp.stack([far, got], axis=1).reshape(-1, *far.shape[1:])
    odd = to_bit(far, HALVING[0])
    direct = to_y(far, -2)
    far = jnp.concatenate([far, odd], axis=0)
    b1, b3 = to_y(far, -1), to_y(far, 1)
    passed = to_y(b1[zl // 2 :], -1)
    far = [far, b1, direct, passed, b3]

    def terms(blocks):
        made = pl.pallas_call(
            terms_kernel,
            out_shape=jax.ShapeDtypeStruct((4 * rows, 3 * LANES), jnp.bfloat16),
            scratch_shapes=[pltpu.VMEM((4 * rows, width), jnp.bfloat16)] * 2,
            name="terms",
        )(*blocks, wide, down)
        made = exchange(made.reshape(8, rows // 2, -1), GZ)
        return total(made)

    def gates(pre):
        gate, upward, dhidden = (pre[:, k * LANES : (k + 1) * LANES] for k in range(3))
        sigmoid = jax.nn.sigmoid(gate)
        hidden = (gate * sigmoid * upward).astype(jnp.bfloat16)
        dgate = (dhidden * upward * sigmoid * (1.0 + gate * (1.0 - sigmoid))).astype(jnp.bfloat16)
        dup = (dhidden * gate * sigmoid).astype(jnp.bfloat16)
        acts = jnp.concatenate([hidden, dgate, dup], axis=1)
        acts = give_all(acts, GZ)
        return acts.reshape(4 * rows, -1)

    def leave(acts):
        parts = pl.pallas_call(leave_kernel, out_shape=[block] * 4, name="leave")(acts, wide, down)
        back = [to_y(parts[d], d) for d in (2, 1, 3)]
        return add(parts[0], *back)

    own_acts = gates(terms(own))
    far_acts = gates(terms(far))
    own_sum = leave(own_acts)
    far_sum = leave(far_acts)
    for k, bit in enumerate(HALVING):
        own_sum, far_sum = (
            halved(*pair, bit)
            for pair in (own_sum, far_sum)
        )
        if k < 2:
            own_sum, far_sum = (
                (a[:, 0], a[:, 1])
                for a in (
                    t.astype(jnp.bfloat16).reshape(-1, 2, *t.shape[1:])
                    for t in (own_sum, far_sum)
                )
            )
    own_sum, far_sum = own_sum[0], far_sum[0].astype(jnp.bfloat16)
    far_sum = across(far_sum)
    ends = (own_sum + far_sum.astype(jnp.float32)).astype(jnp.bfloat16)
    ends = give_all(ends, "zl")
    output, input_grad = (ends[:, k].reshape(rows, width) for k in range(2))

    all_tokens, all_grad = (
        jnp.concatenate([b[:, k].reshape(-1, width) for b in own + far], axis=0)
        for k in range(2)
    )
    acts = jnp.concatenate([own_acts, far_acts], axis=0)
    hidden, dgate, dup = (acts[:, k * LANES : k * LANES + hid] for k in range(3))
    gate_grad = contract_rows(all_tokens, dgate).astype(jnp.bfloat16)
    up_grad = contract_rows(all_tokens, dup).astype(jnp.bfloat16)
    down_grad = contract_rows(hidden, all_grad).astype(jnp.bfloat16)
    return (output, input_grad, gate_grad, up_grad, down_grad)


def solution(mesh):
    finer = Mesh(
        mesh.devices.reshape(4, 2, mesh.shape["gy"], 4, 2), ("y", "zh", "zl", "x", "c")
    )
    gx, ff = ("y", "zh"), ("y", "zh", "zl")
    in_specs = (P(gx, GZ), P(GZ, ff), P(GZ, ff), P(ff, GZ), P(gx, GZ))
    out_specs = (P(gx, GZ), P(gx, GZ), P(GZ, ff), P(GZ, ff), P(ff, GZ))
    return jax.shard_map(work, mesh=finer, in_specs=in_specs, out_specs=out_specs, check_vma=False)
```

```python
import jax
import jax.numpy as jnp
from jax import lax
from jax.experimental import pallas as pl
from jax.experimental.pallas import tpu as pltpu
from jax.sharding import Mesh
from jax.sharding import PartitionSpec as P

GZ = ("x", "c")
Z = ("zh", "zl")
HALVING = (0, 1, 2)
LANES = 256


def give_all(shard, axis):
    devices = lax.axis_size(axis)
    return lax.all_to_all(
        jnp.broadcast_to(shard[None], (devices, *shard.shape)), axis, 0, 0, tiled=True
    )


def exchange(tiles, axis):
    return lax.all_to_all(tiles, axis, 0, 0, tiled=True)


def total(tiles):
    return jnp.sum(tiles.astype(jnp.float32), axis=0)


def to_y(block, d):
    n = lax.axis_size("y")
    return lax.ppermute(block, "y", [(i, (i + d) % n) for i in range(n)])


def of_ys(shard):
    blocks = [shard]
    for d in (1, 2, 3):
        blocks.append(to_y(shard, -d))
    return blocks


def across(shard):
    zl = lax.axis_size("zl")
    nz, step = 2 * zl, zl // 2
    return lax.ppermute(
        shard, Z, [(i, (i - step if i % zl < step else i + step) % nz) for i in range(nz)]
    )


def to_bit(block, bit):
    return lax.ppermute(block, "zl", [(i, i ^ (1 << bit)) for i in range(lax.axis_size("zl"))])


def halved(keep, send, bit):
    got = to_bit(send, bit)
    return keep.astype(jnp.float32) + got.astype(jnp.float32)


def contract_rows(left, right):
    return lax.dot_general(
        left, right, (((0,), (0,)), ((), ())), preferred_element_type=jnp.float32
    )


def contract_cols(left, right):
    return lax.dot_general(
        left, right, (((1,), (1,)), ((), ())), preferred_element_type=jnp.float32
    )


def matmul(left, right):
    return jnp.dot(left, right, preferred_element_type=jnp.float32)


def own_kernel(zl, tokens, grad, out, thin):
    for p, r in enumerate((0, 2, 4, 6, 1, 3, 5, 7)):
        s = jnp.bitwise_xor(zl[0], r)
        out[p, 0] = tokens[s]
        out[p, 1] = grad[s]
    thin[0, 0] = tokens[zl[0]]
    thin[0, 1] = grad[zl[0]]


def terms_kernel(*refs):
    *blocks, wide, down, out, t, g = refs
    at = 0
    for b in blocks:
        n, _, cut, width = b.shape
        rows = pl.ds(at, n * cut)
        t[rows] = b[:, 0].reshape(n * cut, width)
        g[rows] = b[:, 1].reshape(n * cut, width)
        at += n * cut
    out[:, : 2 * LANES] = contract_cols(t[...], wide[...]).astype(jnp.bfloat16)
    out[:, 2 * LANES :] = contract_cols(g[...], down[...]).astype(jnp.bfloat16)


def leave_kernel(acts, wide, down, *outs):
    o = matmul(acts[:, :LANES], down[...]).astype(jnp.bfloat16)
    i = matmul(acts[:, LANES:], wide[...]).astype(jnp.bfloat16)
    at = 0
    for out in outs:
        n, _, cut, width = out.shape
        out[:, 0] = o[at : at + n * cut].reshape(n, cut, width)
        out[:, 1] = i[at : at + n * cut].reshape(n, cut, width)
        at += n * cut


def sum_kernel(*refs):
    *terms, even, odd = refs
    half = even.shape[0]
    for out, at in ((even, 0), (odd, half)):
        rows = pl.ds(at, half)
        out[...] = sum(t[rows].astype(jnp.float32) for t in terms).astype(jnp.bfloat16)


def add(*terms):
    n, *rest = terms[0].shape
    shape = jax.ShapeDtypeStruct((n // 2, *rest), jnp.bfloat16)
    return pl.pallas_call(sum_kernel, out_shape=[shape] * 2, name="add")(*terms)


def work(tokens, gate_weight, up_weight, down_weight, out_grad):
    rows, width = tokens.shape
    hid = down_weight.shape[0]
    zl = lax.axis_size("zl")
    cut = rows // zl
    block = jax.ShapeDtypeStruct((zl, 2, cut, width), jnp.bfloat16)
    more = LANES - hid
    vmem = pl.BlockSpec(memory_space=pltpu.VMEM)
    own, thin = pl.pallas_call(
        own_kernel,
        out_shape=[block, jax.ShapeDtypeStruct((1, *block.shape[1:]), jnp.bfloat16)],
        in_specs=[pl.BlockSpec(memory_space=pltpu.SMEM), vmem, vmem],
        name="own",
    )(
        lax.axis_index("zl").astype(jnp.int32).reshape(1),
        *(a.reshape(zl, cut, width) for a in (tokens, out_grad)),
    )
    wide = jnp.concatenate(
        [jnp.pad(w.T, ((0, more), (0, 0))) for w in (gate_weight, up_weight)], axis=0
    )
    down = jnp.pad(down_weight, ((0, more), (0, 0)))
    far = across(thin)
    own = of_ys(own)
    for bit in HALVING[:0:-1]:
        got = to_bit(far, bit)
        far = jnp.stack([far, got], axis=1).reshape(-1, *far.shape[1:])
    odd = to_bit(far, HALVING[0])
    direct = to_y(far, -2)
    far = jnp.concatenate([far, odd], axis=0)
    b1, b3 = to_y(far, -1), to_y(far, 1)
    passed = to_y(b1[zl // 2 :], -1)
    far = [far, b1, direct, passed, b3]

    def terms(blocks):
        made = pl.pallas_call(
            terms_kernel,
            out_shape=jax.ShapeDtypeStruct((4 * rows, 3 * LANES), jnp.bfloat16),
            scratch_shapes=[pltpu.VMEM((4 * rows, width), jnp.bfloat16)] * 2,
            name="terms",
        )(*blocks, wide, down)
        made = exchange(made.reshape(8, rows // 2, -1), GZ)
        return total(made)

    def gates(pre):
        gate, upward, dhidden = (pre[:, k * LANES : (k + 1) * LANES] for k in range(3))
        sigmoid = jax.nn.sigmoid(gate)
        hidden = (gate * sigmoid * upward).astype(jnp.bfloat16)
        dgate = (dhidden * upward * sigmoid * (1.0 + gate * (1.0 - sigmoid))).astype(jnp.bfloat16)
        dup = (dhidden * gate * sigmoid).astype(jnp.bfloat16)
        acts = jnp.concatenate([hidden, dgate, dup], axis=1)
        acts = give_all(acts, GZ)
        return acts.reshape(4 * rows, -1)

    def leave(acts):
        parts = pl.pallas_call(leave_kernel, out_shape=[block] * 4, name="leave")(acts, wide, down)
        back = [to_y(parts[d], d) for d in (2, 1, 3)]
        return add(parts[0], *back)

    own_acts = gates(terms(own))
    far_acts = gates(terms(far))
    own_sum = leave(own_acts)
    far_sum = leave(far_acts)
    for k, bit in enumerate(HALVING):
        own_sum, far_sum = (
            halved(*pair, bit)
            for pair in (own_sum, far_sum)
        )
        if k < 2:
            own_sum, far_sum = (
                (a[:, 0], a[:, 1])
                for a in (
                    t.astype(jnp.bfloat16).reshape(-1, 2, *t.shape[1:])
                    for t in (own_sum, far_sum)
                )
            )
    own_sum, far_sum = own_sum[0], far_sum[0].astype(jnp.bfloat16)
    far_sum = across(far_sum)
    ends = (own_sum + far_sum.astype(jnp.float32)).astype(jnp.bfloat16)
    ends = give_all(ends, "zl")
    output, input_grad = (ends[:, k].reshape(rows, width) for k in range(2))

    all_tokens, all_grad = (
        jnp.concatenate([b[:, k].reshape(-1, width) for b in own + far], axis=0)
        for k in range(2)
    )
    acts = jnp.concatenate([own_acts, far_acts], axis=0)
    hidden, dgate, dup = (acts[:, k * LANES : k * LANES + hid] for k in range(3))
    gate_grad = contract_rows(all_tokens, dgate).astype(jnp.bfloat16)
    up_grad = contract_rows(all_tokens, dup).astype(jnp.bfloat16)
    down_grad = contract_rows(hidden, all_grad).astype(jnp.bfloat16)
    return (output, input_grad, gate_grad, up_grad, down_grad)


def solution(mesh):
    finer = Mesh(
        mesh.devices.reshape(4, 2, mesh.shape["gy"], 4, 2), ("y", "zh", "zl", "x", "c")
    )
    gx, ff = ("y", "zh"), ("y", "zh", "zl")
    in_specs = (P(gx, GZ), P(GZ, ff), P(GZ, ff), P(ff, GZ), P(gx, GZ))
    out_specs = (P(gx, GZ), P(gx, GZ), P(GZ, ff), P(GZ, ff), P(ff, GZ))
    return jax.shard_map(work, mesh=finer, in_specs=in_specs, out_specs=out_specs, check_vma=False)
```
